512 devices in a mesh: dp: 32 (over x, y, core), expert: 16 (over z).
Axes of the slice: x: 4, y: 4, z: 16, core: 2. Of those that a mesh axis runs over, the one named last changes fastest.
Arguments:
- tokens: bfloat16 [65536, 7168], P(('dp', 'expert')), may hold values from -6 to 6
- route_ids: int32 [65536, 8], P(('dp', 'expert')), may hold values from 0 to 255, as said below
- route_gates: float32 [65536, 8], P(('dp', 'expert')), may hold values from 0.1 to 1
- gate_up: bfloat16 [2, 7168, 2048], P(None, 'dp', 'expert'), may hold values from -0.0625 to 0.0625
- down_weight: bfloat16 [2048, 7168], P('expert', 'dp'), may hold values from -0.125 to 0.125
Outputs:
- mixed: bfloat16 [65536, 7168], P(('dp', 'expert'))
The draws below stay inside these ranges and needn't reach their ends.
Inputs may be any that keep to these rules, and one draw needn't show every extreme that they name: `route_ids`: each token names 8 different experts. Among the 128 rows of one device, each expert below 1 is named by 1 to 12 rows; for each such expert, in every draw some run of 16 consecutive devices' blocks (aligned at multiples of 16) has exactly 12 rows naming it in every block.
All inputs are finite; a program needn't handle non-finite values.
Results may differ from the reference program's by a relative error of at most 0.0057.
Values may be sent and summed in bfloat16 or wider, within the bound.
No kernel may reach another device: no remote copies, remote signals or barrier semaphores. Data moves between devices by JAX's collectives and lax.ppermute only.
A program may use at most 64 MiB of HBM per device.

```python
import jax
import jax.numpy as jnp
from jax import lax

D = 7168
FF = 2048
ROUTED = 256
TOPK = 8
EXPERTS = 1
TOK_DEV = 128
CAP = 12
TOKENS = 65536
N_EXPERT = 16


def draw_route_ids(key, part):
    blocks = TOKENS // TOK_DEV
    subkeys = jax.random.split(key, 7)
    counts = jax.random.randint(subkeys[0], (blocks, EXPERTS), 1, CAP + 1)
    full_group = jax.random.randint(subkeys[1], (EXPERTS,), 0, blocks // N_EXPERT)
    group_of = jnp.arange(blocks, dtype=jnp.int32) // N_EXPERT
    counts = jnp.where(group_of[:, None] == full_group[None, :], CAP, counts)
    scores = jax.random.randint(subkeys[2], (blocks, EXPERTS, TOK_DEV), 0, 1 << 20) * TOK_DEV + jnp.arange(TOK_DEV, dtype=jnp.int32)[None, None, :]
    ranking = jnp.argsort(jnp.argsort(scores, axis=2), axis=2)
    chosen = ranking < counts[:, :, None]
    offsets = jax.random.randint(subkeys[3], (blocks, TOK_DEV, 1), 0, ROUTED - EXPERTS)
    stride = 2 * jax.random.randint(subkeys[4], (blocks, TOK_DEV, 1), 0, 16) + 1
    slot_ids = jnp.arange(TOPK, dtype=jnp.int32)[None, None, :]
    others = EXPERTS + (offsets + slot_ids * stride) % (ROUTED - EXPERTS)
    leading = jax.random.randint(subkeys[5], (blocks, TOK_DEV, 1), 0, TOPK)
    spacing = 1 + jax.random.randint(subkeys[6], (blocks, TOK_DEV, 1), 0, TOPK - 1)
    result = others
    for expert in range(EXPERTS):
        position = (leading + expert * spacing) % TOPK
        result = jnp.where((slot_ids == position) & chosen[:, expert, :, None], expert, result)
    return result.reshape(blocks * TOK_DEV, TOPK).astype(jnp.int32)


def shard_levels(key, dims, cuts, least, high):
    def one(axis_at, blocks):
        steps = jax.random.uniform(jax.random.fold_in(jax.random.fold_in(key, 6), axis_at), (blocks,), jnp.float32, least / len(cuts), high / len(cuts))
        return jnp.repeat(jnp.exp(steps), dims[axis_at] // blocks).reshape((-1,) + (1,) * (len(dims) - axis_at - 1))

    gain = one(*cuts[0])
    for cut in cuts[1:]:
        gain = gain * one(*cut)
    return gain


def gaussian(stream_key, extent, width, reach, cuts=(), held_as=jnp.bfloat16):
    values = width * jax.random.normal(stream_key, extent, jnp.float32)
    if cuts:
        values = values * shard_levels(stream_key, extent, cuts, -0.22, 0.18)
    return jnp.clip(values, -reach, reach).astype(held_as)


def setup_inputs(seed: int = 0) -> dict:
    key_of = jax.random.split(jax.random.key(seed), 6)
    tokens = gaussian(key_of[0], (TOKENS, D), 1.0, 6.0, ((0, 512),))
    route_ids = draw_route_ids(jax.random.fold_in(key_of[5], 71), 0)
    route_gates = jnp.clip(0.1 + 0.9 * jax.random.uniform(key_of[2], (TOKENS, TOPK), jnp.float32) ** shard_levels(key_of[2], (TOKENS, TOPK), ((0, 512),), -0.2, 0.2), 0.1, 1.0)
    gate_up = gaussian(key_of[3], (2, D, EXPERTS * FF), D ** -0.5, 0.0625, ((1, 32), (2, 16)))
    down_weight = gaussian(key_of[4], (EXPERTS * FF, D), FF ** -0.5, 0.125, ((0, 16), (1, 32)))
    return dict(tokens=tokens, route_ids=route_ids, route_gates=route_gates, gate_up=gate_up, down_weight=down_weight)


def reference(tokens, route_ids, route_gates, gate_up, down_weight):
    slices = N_EXPERT // EXPERTS
    slice_width = FF // slices
    blocks = TOKENS // TOK_DEV
    grouped_ids = route_ids.reshape(blocks, TOK_DEV, TOPK)
    grouped_gates = route_gates.reshape(blocks, TOK_DEV, TOPK)
    grouped = tokens.reshape(blocks, TOK_DEV, D)
    capacity_ids = jnp.arange(CAP, dtype=jnp.int32)
    token_ids = jnp.arange(TOK_DEV, dtype=jnp.int32)
    outputs = []
    routed_all = []
    places_all = []
    weights_all = []
    for expert in range(EXPERTS):
        matches = grouped_ids == expert
        routed = jnp.any(matches, axis=2)
        weight = jnp.sum(jnp.where(matches, grouped_gates, jnp.float32(0.0)), axis=2).astype(jnp.float32)
        places = (jnp.cumsum(routed.astype(jnp.int32), axis=1) - 1).astype(jnp.int32)
        chosen = routed[:, None, :] & (places[:, None, :] == capacity_ids[None, :, None])
        source_rows = jnp.sum(jnp.where(chosen, token_ids[None, None, :], 0), axis=2).astype(jnp.int32)
        selected = jnp.take_along_axis(grouped, source_rows[:, :, None], axis=1).reshape(blocks * CAP, D)
        gate_proj = jnp.dot(selected, gate_up[0][:, expert * FF:(expert + 1) * FF], preferred_element_type=jnp.float32)
        up_proj = jnp.dot(selected, gate_up[1][:, expert * FF:(expert + 1) * FF], preferred_element_type=jnp.float32)
        hidden = (jax.nn.silu(gate_proj) * up_proj).astype(jnp.bfloat16)
        running = jnp.zeros((blocks * CAP, D), jnp.float32)
        for piece_index in range(slices):
            lower = piece_index * slice_width
            rows_down = down_weight[expert * FF + lower:expert * FF + lower + slice_width, :]
            partial_value = jnp.dot(hidden[:, lower:lower + slice_width], rows_down, preferred_element_type=jnp.float32).astype(jnp.bfloat16)
            running = running + partial_value.astype(jnp.float32)
        outputs.append(running.reshape(blocks, CAP, D))
        routed_all.append(routed)
        places_all.append(jnp.clip(places, 0, CAP - 1).astype(jnp.int32))
        weights_all.append(weight)
    stacked_out = jnp.stack(outputs, axis=1)
    stacked_routed = jnp.stack(routed_all, axis=1)
    stacked_places = jnp.stack(places_all, axis=1)
    stacked_weights = jnp.stack(weights_all, axis=1)

    def assemble(inputs):
        expert_out, routed, places, weight = inputs
        mixed_block = jnp.zeros((TOK_DEV, D), jnp.float32)
        for expert in range(EXPERTS):
            picked = jnp.take(expert_out[expert], places[expert], axis=0)
            mixed_block = mixed_block + jnp.where(routed[expert][:, None], weight[expert][:, None] * picked, jnp.float32(0.0))
        return mixed_block.astype(jnp.bfloat16)

    mixed = lax.map(assemble, (stacked_out, stacked_routed, stacked_places, stacked_weights))
    return mixed.reshape(TOKENS, D)
```

```python
import jax
import jax.numpy as jnp
from jax import lax
from jax.sharding import PartitionSpec as P

EXPERTS = 1
CAP = 12


def body(tokens, route_ids, route_gates, gate_up, down_weight):
    model_width = tokens.shape[1]
    matches = route_ids == 0
    routed = jnp.any(matches, axis=1)
    weight = jnp.sum(jnp.where(matches, route_gates, 0.0), axis=1)
    places = jnp.cumsum(routed.astype(jnp.int32)) - 1
    capacity_ids = jnp.arange(CAP, dtype=jnp.int32)
    packing = (routed[None, :] & (places[None, :] == capacity_ids[:, None])).astype(jnp.bfloat16)
    packed = jnp.dot(packing, tokens, preferred_element_type=jnp.float32).astype(jnp.bfloat16)
    dispatched = lax.all_gather(packed, "expert", axis=0, tiled=True)
    gu = lax.all_gather(gate_up, "dp", axis=1, tiled=True)
    dn = lax.all_gather(down_weight, "dp", axis=1, tiled=True)
    projected = jnp.einsum("rd,gdf->grf", dispatched, gu, preferred_element_type=jnp.float32)
    hidden = (jax.nn.silu(projected[0]) * projected[1]).astype(jnp.bfloat16)
    partial_value = jnp.dot(hidden, dn, preferred_element_type=jnp.float32).astype(jnp.bfloat16)
    summed = lax.psum_scatter(partial_value, "expert", scatter_dimension=0, tiled=True)
    selector = routed[:, None] & (places[:, None] == capacity_ids[None, :])
    scaled = jnp.where(selector, weight[:, None], 0.0)
    mixed = jnp.dot(
        scaled, summed.astype(jnp.float32), precision=lax.Precision.HIGHEST, preferred_element_type=jnp.float32
    )
    return mixed.astype(jnp.bfloat16)


def solution(mesh):
    return jax.shard_map(
        body,
        mesh=mesh,
        in_specs=(
            P(("dp", "expert"), None),
            P(("dp", "expert"), None),
            P(("dp", "expert"), None),
            P(None, "dp", "expert"),
            P("expert", "dp"),
        ),
        out_specs=P(("dp", "expert"), None),
        check_vma=False,
    )
```

```python
import functools

import jax
import jax.numpy as jnp
from jax import lax
from jax.experimental import pallas as pl
from jax.experimental.pallas import tpu as pltpu
from jax.sharding import PartitionSpec as P


CAP = 12
SLOT = 16
COLS = 1024
STEPS = (0, 1, 3, 2)


def plane_routes(axis, step):
    routes = []
    for x in range(4):
        for y in range(4):
            for core in range(2):
                source = ((x + step) % 4, y) if axis == "x" else (x, (y + step) % 4)
                routes.append((source[0] * 8 + source[1] * 2 + core, x * 8 + y * 2 + core))
    return routes


def gather_ring(block, axis):
    return [block] + [lax.ppermute(block, "dp", plane_routes(axis, s)) for s in STEPS[1:]]


def ffn_kernel(pos_ref, tokens_ref, own_ref, other_ref, out_ref, weights, rows, sums, sem):
    members, cap, model_width = tokens_ref.shape
    hidden_width = weights.shape[2]
    half = own_ref.shape[4]
    x, y, core = pos_ref[0], pos_ref[1], pos_ref[2]
    for source, side in ((own_ref, core), (other_ref, 1 - core)):
        for part in range(2):
            for k, outer in enumerate(STEPS):
                for i, inner in enumerate(STEPS):
                    dx, dy = (inner, outer) if part == 0 else (outer, inner)
                    place = lax.rem(x + dx, 4) * 8 + lax.rem(y + dy, 4) * 2 + side
                    start = pl.multiple_of(place * (2 * half) + part * half, 16)
                    pltpu.make_async_copy(
                        source.at[part, k, i], weights.at[:, pl.ds(start, half), :], sem
                    ).start()
    for s in range(members):
        rows[s * SLOT : s * SLOT + cap, :] = tokens_ref[s]
    pltpu.make_async_copy(weights, weights, sem).wait()

    chunk = 1024
    gate = jnp.zeros((members * SLOT, hidden_width), jnp.float32)
    up = jnp.zeros((members * SLOT, hidden_width), jnp.float32)
    for j in range(model_width // chunk):
        part = slice(j * chunk, (j + 1) * chunk)
        gate += jnp.dot(rows[:, part], weights[0, part, :], preferred_element_type=jnp.float32)
        up += jnp.dot(rows[:, part], weights[1, part, :], preferred_element_type=jnp.float32)
    hidden = (gate / (1.0 + jnp.exp(-gate)) * up).astype(jnp.bfloat16)
    stride = out_ref.shape[0] // members
    blocks = model_width // COLS
    for j in range(blocks):
        result = lax.dot_general(
            hidden,
            weights[2, j * COLS : (j + 1) * COLS, :],
            (((1,), (1,)), ((), ())),
            preferred_element_type=jnp.float32,
        )
        for s in range(members):
            first = s * stride + j * cap
            sums[first : first + cap, :] = result[s * SLOT : s * SLOT + cap, :]
    for s in range(members):
        sums[s * stride + blocks * cap : (s + 1) * stride, :] = jnp.zeros(
            (stride - blocks * cap, COLS), jnp.float32
        )
    for r in range(0, out_ref.shape[0], 48):
        out_ref[r : r + 48, :] = sums[r : r + 48, :].astype(jnp.bfloat16)


def ffn(position, gathered, own, other):
    members, cap, model_width = gathered.shape
    used = model_width // COLS * cap
    stride = used // 8 * 8 + 7
    total = members * stride
    vmem = pl.BlockSpec(memory_space=pltpu.VMEM)
    anywhere = pl.BlockSpec(memory_space=pl.ANY)
    return pl.pallas_call(
        ffn_kernel,
        out_shape=jax.ShapeDtypeStruct((total, COLS), jnp.bfloat16),
        in_specs=[pl.BlockSpec(memory_space=pltpu.SMEM), vmem, anywhere, anywhere],
        out_specs=vmem,
        scratch_shapes=[
            pltpu.VMEM((3, model_width, own.shape[-1]), jnp.bfloat16),
            pltpu.VMEM((members * SLOT, model_width), jnp.bfloat16),
            pltpu.VMEM((total, COLS), jnp.float32),
            pltpu.SemaphoreType.DMA,
        ],
        compiler_params=pltpu.CompilerParams(vmem_limit_bytes=48 << 20),
        cost_estimate=pl.CostEstimate(
            flops=6 * members * SLOT * model_width * own.shape[-1],
            bytes_accessed=14 << 20,
            transcendentals=members * SLOT * own.shape[-1],
        ),
    )(position, gathered, own, other)


def body(tokens, route_ids, route_gates, gate_up, down_weight):
    model_width = tokens.shape[1]
    matches = route_ids == 0
    routed = jnp.any(matches, axis=1)
    weight = jnp.sum(jnp.where(matches, route_gates, 0.0), axis=1)
    places = jnp.cumsum(routed.astype(jnp.int32)) - 1
    capacity_ids = jnp.arange(CAP, dtype=jnp.int32)
    packing = (routed[None, :] & (places[None, :] == capacity_ids[:, None])).astype(jnp.bfloat16)
    packed = jnp.dot(packing, tokens, preferred_element_type=jnp.float32).astype(jnp.bfloat16)
    gathered = lax.all_gather(packed, "expert", axis=0, tiled=False)

    shard = jnp.concatenate((gate_up, down_weight.T[None]), axis=0)
    half = shard.shape[1] // 2
    first = jnp.stack(gather_ring(shard[:, :half], "x"))
    second = jnp.stack(gather_ring(shard[:, half:], "y"))
    first = jnp.stack(gather_ring(first, "y"))
    second = jnp.stack(gather_ring(second, "x"))
    own = jnp.stack((first, second))
    other = lax.ppermute(own, "dp", [(i, i ^ 1) for i in range(32)])

    dp = lax.axis_index("dp")
    position = jnp.stack((dp // 8, dp // 2 % 4, dp % 2)).astype(jnp.int32)
    partial_value = ffn(position, gathered, own, other)
    summed = lax.psum_scatter(partial_value, "expert", scatter_dimension=0, tiled=True)
    summed = lax.optimization_barrier(summed)
    blocks = model_width // COLS
    summed = summed[: blocks * CAP].reshape(blocks, CAP, COLS)
    summed = jnp.transpose(summed, (1, 0, 2)).reshape(CAP, model_width)
    selector = routed[:, None] & (places[:, None] == capacity_ids[None, :])
    scaled = jnp.where(selector, weight[:, None], 0.0)
    mixed = jnp.dot(
        scaled,
        summed.astype(jnp.float32),
        precision=lax.Precision.HIGHEST,
        preferred_element_type=jnp.float32,
    )
    return mixed.astype(jnp.bfloat16)


def solution(mesh):
    return jax.shard_map(
        body,
        mesh=mesh,
        in_specs=(
            P(("dp", "expert"), None),
            P(("dp", "expert"), None),
            P(("dp", "expert"), None),
            P(None, "dp", "expert"),
            P("expert", "dp"),
        ),
        out_specs=P(("dp", "expert"), None),
        check_vma=False,
    )
```

```python
import functools

import jax
import jax.numpy as jnp
from jax import lax
from jax.experimental import pallas as pl
from jax.experimental.pallas import tpu as pltpu
from jax.sharding import PartitionSpec as P


CAP = 12
SLOT = 16
COLS = 1024
STEPS = (0, 1, 3, 2)


def swap_cores(block):
    return lax.ppermute(block, "dp", [(i, i ^ 1) for i in range(32)])


def turn_plane(block, step, flip):
    routes = []
    for x in range(4):
        for y in range(4):
            for core in range(2):
                along_x = (core == 0) != flip
                source = ((x + step) % 4, y) if along_x else (x, (y + step) % 4)
                routes.append((source[0] * 8 + source[1] * 2 + core, x * 8 + y * 2 + core))
    return lax.ppermute(block, "dp", routes)


def turn_column(block, members):
    routes = []
    for dp in range(32):
        for z in range(members):
            after = (z + (1 if dp % 2 == 0 else -1)) % members
            routes.append((dp * members + z, dp * members + after))
    return lax.ppermute(block, ("dp", "expert"), routes)


def after(value, event):
    return lax.optimization_barrier((value, event))


def ffn_kernel(pos_ref, *refs):
    token_refs, (own_ref, other_ref, out_ref, weights, rows, sums, sem) = refs[:-7], refs[-7:]
    model_width, hidden_width = weights.shape[1:]
    members = rows.shape[0] // SLOT
    half = own_ref.shape[4]
    half_width = model_width // 2
    x, y, core, z = pos_ref[0], pos_ref[1], pos_ref[2], pos_ref[3]
    for source, holder in ((own_ref, core), (other_ref, 1 - core)):
        for k, outer in enumerate(STEPS):
            for i, inner in enumerate(STEPS):
                for side in range(2):
                    dx = inner + holder * (outer - inner)
                    dy = outer + holder * (inner - outer)
                    bit = holder + side - 2 * holder * side
                    place = lax.rem(x + dx, 4) * 8 + lax.rem(y + dy, 4) * 2 + bit
                    start = pl.multiple_of(place * (2 * half) + holder * half, 16)
                    pltpu.make_async_copy(
                        source.at[k, i, side], weights.at[:, pl.ds(start, half), :], sem
                    ).start()

    def place_rows(block, plane):
        start = pl.multiple_of(plane * SLOT, SLOT)
        rows[pl.ds(start, CAP), :half_width] = block[:CAP]
        rows[pl.ds(start, CAP), half_width:] = block[CAP:]

    toward = 2 * core - 1
    mine, last = token_refs[:members // 2], token_refs[members // 2]
    swapped = token_refs[members // 2 + 1 :]
    for k, ref in enumerate(mine):
        place_rows(ref[: 2 * CAP], lax.rem(z + k * toward + members, members))
    place_rows(last[...], lax.rem(z + members // 2, members))
    k = 1
    for ref in swapped:
        for first in range(0, ref.shape[0], 2 * CAP):
            place_rows(ref[first : first + 2 * CAP], lax.rem(z - k * toward + members, members))
            k += 1
    pltpu.make_async_copy(weights, weights, sem).wait()

    chunk = 1024
    gate = jnp.zeros((members * SLOT, hidden_width), jnp.float32)
    up = jnp.zeros((members * SLOT, hidden_width), jnp.float32)
    for j in range(model_width // chunk):
        part = slice(j * chunk, (j + 1) * chunk)
        gate += jnp.dot(rows[:, part], weights[0, part, :], preferred_element_type=jnp.float32)
        up += jnp.dot(rows[:, part], weights[1, part, :], preferred_element_type=jnp.float32)
    hidden = (gate / (1.0 + jnp.exp(-gate)) * up).astype(jnp.bfloat16)
    stride = out_ref.shape[0] // members
    blocks = model_width // COLS
    for j in range(blocks):
        result = lax.dot_general(
            hidden,
            weights[2, j * COLS : (j + 1) * COLS, :],
            (((1,), (1,)), ((), ())),
            preferred_element_type=jnp.float32,
        )
        for s in range(members):
            first = s * stride + j * CAP
            sums[first : first + CAP, :] = result[s * SLOT : s * SLOT + CAP, :]
    for s in range(members):
        sums[s * stride + blocks * CAP : (s + 1) * stride, :] = jnp.zeros(
            (stride - blocks * CAP, COLS), jnp.float32
        )
    for r in range(0, out_ref.shape[0], 48):
        out_ref[r : r + 48, :] = sums[r : r + 48, :].astype(jnp.bfloat16)


def ffn(position, blocks, own, other, members, model_width):
    used = model_width // COLS * CAP
    stride = used // 8 * 8 + 7
    total = members * stride
    vmem = pl.BlockSpec(memory_space=pltpu.VMEM)
    anywhere = pl.BlockSpec(memory_space=pl.ANY)
    return pl.pallas_call(
        ffn_kernel,
        out_shape=jax.ShapeDtypeStruct((total, COLS), jnp.bfloat16),
        in_specs=[pl.BlockSpec(memory_space=pltpu.SMEM)] + [vmem] * len(blocks) + [anywhere] * 2,
        out_specs=vmem,
        scratch_shapes=[
            pltpu.VMEM((3, model_width, own.shape[-1]), jnp.bfloat16),
            pltpu.VMEM((members * SLOT, model_width), jnp.bfloat16),
            pltpu.VMEM((total, COLS), jnp.float32),
            pltpu.SemaphoreType.DMA,
        ],
        compiler_params=pltpu.CompilerParams(vmem_limit_bytes=40 << 20),
        cost_estimate=pl.CostEstimate(
            flops=6 * members * SLOT * model_width * own.shape[-1],
            bytes_accessed=14 << 20,
            transcendentals=members * SLOT * own.shape[-1],
        ),
    )(position, *blocks, own, other)


def body(tokens, route_ids, route_gates, gate_up, down_weight):
    members = lax.axis_size("expert")
    model_width = tokens.shape[1]
    dp, z = lax.axis_index("dp"), lax.axis_index("expert")
    core = dp % 2

    shard = jnp.concatenate((gate_up, down_weight.T[None]), axis=0)
    half = shard.shape[1] // 2
    kept = lax.dynamic_slice_in_dim(shard, core * half, half, axis=1)
    given = lax.dynamic_slice_in_dim(shard, (1 - core) * half, half, axis=1)
    weights = jnp.stack((kept, swap_cores(given)))

    matches = route_ids == 0
    routed = jnp.any(matches, axis=1)
    weight = jnp.sum(jnp.where(matches, route_gates, 0.0), axis=1)
    places = jnp.cumsum(routed.astype(jnp.int32)) - 1
    capacity_ids = jnp.arange(CAP, dtype=jnp.int32)
    packing = (routed[None, :] & (places[None, :] == capacity_ids[:, None])).astype(jnp.bfloat16)
    packed = jnp.dot(packing, tokens, preferred_element_type=jnp.float32).astype(jnp.bfloat16)
    packed = jnp.concatenate((packed[:, : model_width // 2], packed[:, model_width // 2 :]), axis=0)

    pair = jnp.concatenate((packed, swap_cores(packed)), axis=0)
    mine = [pair]
    pieces = [weights]
    rank = 2 * CAP
    own = other = None
    swapped = []
    for k in range(1, members // 2 + 1):
        event = mine[-1]
        if k <= 3:
            ready, event = after(weights, event)
            pieces.append(turn_plane(ready, STEPS[k], False))
        if k == 4:
            weights = jnp.stack(pieces)
            pieces = [weights]
        if 4 <= k <= 6:
            ready, event = after(weights, event)
            pieces.append(turn_plane(ready, STEPS[(3, 1, 2)[k - 4]], True))
        if k == 6:
            ready, event = after(jnp.concatenate([m[rank:] for m in mine[1:5]]), event)
            swapped.append(swap_cores(ready))
        if k == 8:
            own = jnp.stack((pieces[0], pieces[2], pieces[3], pieces[1]))
            ready, event = after(own, event)
            other = swap_cores(ready)
            ready, event = after(jnp.concatenate([m[rank:] for m in mine[5:8]]), event)
            swapped.append(swap_cores(ready))
            last = turn_column(event[:rank], members)
        else:
            mine.append(turn_column(event, members))

    position = jnp.stack((dp // 8, dp // 2 % 4, core, z)).astype(jnp.int32)
    partial_value = ffn(position, (*mine, last, *swapped), own, other, members, model_width)
    summed = lax.psum_scatter(partial_value, "expert", scatter_dimension=0, tiled=True)
    summed = lax.optimization_barrier(summed)
    blocks = model_width // COLS
    summed = summed[: blocks * CAP].reshape(blocks, CAP, COLS)
    summed = jnp.transpose(summed, (1, 0, 2)).reshape(CAP, model_width)
    selector = routed[:, None] & (places[:, None] == capacity_ids[None, :])
    scaled = jnp.where(selector, weight[:, None], 0.0)
    mixed = jnp.dot(
        scaled,
        summed.astype(jnp.float32),
        precision=lax.Precision.HIGHEST,
        preferred_element_type=jnp.float32,
    )
    return mixed.astype(jnp.bfloat16)


def solution(mesh):
    return jax.shard_map(
        body,
        mesh=mesh,
        in_specs=(
            P(("dp", "expert"), None),
            P(("dp", "expert"), None),
            P(("dp", "expert"), None),
            P(None, "dp", "expert"),
            P("expert", "dp"),
        ),
        out_specs=P(("dp", "expert"), None),
        check_vma=False,
    )
```

```python
import functools

import jax
import jax.numpy as jnp
from jax import lax
from jax.experimental import pallas as pl
from jax.experimental.pallas import tpu as pltpu
from jax.sharding import PartitionSpec as P


CAP = 12
SLOT = 16
FAR = 2304
COLS = 1024
STEPS = (0, 1, 3, 2)


def swap_cores(block):
    return lax.ppermute(block, "dp", [(i, i ^ 1) for i in range(32)])


def turn_plane(block, step, flip):
    routes = []
    for x in range(4):
        for y in range(4):
            for core in range(2):
                along_x = (core == 0) != flip
                source = ((x + step) % 4, y) if along_x else (x, (y + step) % 4)
                routes.append((source[0] * 8 + source[1] * 2 + core, x * 8 + y * 2 + core))
    return lax.ppermute(block, "dp", routes)


def ffn_kernel(
    pos_ref, far_ref, near_ref, own_ref, other_ref, out_ref,
    far, near, wide, down, rows, sums, far_sem, near_sem, wide_sem, down_sem,
):
    model_width, hidden_width = down.shape
    half = own_ref.shape[4]
    far_width, near_width = far.shape[1], near.shape[1]
    members = far.shape[0] // (2 * CAP)
    pltpu.make_async_copy(far_ref, far, far_sem).start()
    pltpu.make_async_copy(near_ref, near, near_sem).start()
    x, y, core = pos_ref[0], pos_ref[1], pos_ref[2]
    for source, holder in ((own_ref, core), (other_ref, 1 - core)):
        for k, outer in enumerate(STEPS):
            for i, inner in enumerate(STEPS):
                for side in range(2):
                    dx = inner + holder * (outer - inner)
                    dy = outer + holder * (inner - outer)
                    bit = holder + side - 2 * holder * side
                    place = lax.rem(x + dx, 4) * 8 + lax.rem(y + dy, 4) * 2 + bit
                    start = pl.multiple_of(place * (2 * half) + holder * half, 16)
                    for part in range(2):
                        lanes = slice(part * hidden_width, (part + 1) * hidden_width)
                        pltpu.make_async_copy(
                            source.at[k, i, side, part],
                            wide.at[pl.ds(start, half), lanes],
                            wide_sem,
                        ).start()
                    pltpu.make_async_copy(
                        source.at[k, i, side, 2], down.at[pl.ds(start, half), :], down_sem
                    ).start()

    def fill(source_ref, first, width):
        for s in range(members):
            for h in range(2):
                start = h * (far_width + near_width) + first
                rows[s * SLOT : s * SLOT + CAP, start : start + width] = source_ref[
                    (2 * s + h) * CAP : (2 * s + h + 1) * CAP, :
                ]

    pltpu.make_async_copy(near_ref, near, near_sem).wait()
    fill(near, far_width, near_width)
    pltpu.make_async_copy(far_ref, far, far_sem).wait()
    fill(far, 0, far_width)
    pltpu.make_async_copy(wide, wide, wide_sem).wait()
    chunk = 1024
    both = jnp.zeros((members * SLOT, 2 * hidden_width), jnp.float32)
    for j in range(model_width // chunk):
        part = slice(j * chunk, (j + 1) * chunk)
        both += jnp.dot(rows[:, part], wide[part, :], preferred_element_type=jnp.float32)
    gate, up = both[:, :hidden_width], both[:, hidden_width:]
    hidden = (gate / (1.0 + jnp.exp(-gate)) * up).astype(jnp.bfloat16)
    pltpu.make_async_copy(down, down, down_sem).wait()
    stride = out_ref.shape[0] // members
    blocks = model_width // COLS
    for j in range(blocks):
        result = lax.dot_general(
            hidden,
            down[j * COLS : (j + 1) * COLS, :],
            (((1,), (1,)), ((), ())),
            preferred_element_type=jnp.float32,
        )
        for s in range(members):
            first = s * stride + j * CAP
            sums[first : first + CAP, :] = result[s * SLOT : s * SLOT + CAP, :]
    for s in range(members):
        sums[s * stride + blocks * CAP : (s + 1) * stride, :] = jnp.zeros(
            (stride - blocks * CAP, COLS), jnp.float32
        )
    for r in range(0, out_ref.shape[0], 48):
        out_ref[r : r + 48, :] = sums[r : r + 48, :].astype(jnp.bfloat16)


def ffn(position, far, near, own, other):
    width = own.shape[-1]
    model_width = 2 * (far.shape[1] + near.shape[1])
    members = far.shape[0] // (2 * CAP)
    used = model_width // COLS * CAP
    stride = used // 8 * 8 + 7
    total = members * stride
    anywhere = pl.BlockSpec(memory_space=pl.ANY)
    return pl.pallas_call(
        ffn_kernel,
        out_shape=jax.ShapeDtypeStruct((total, COLS), jnp.bfloat16),
        in_specs=[pl.BlockSpec(memory_space=pltpu.SMEM)] + [anywhere] * 4,
        out_specs=pl.BlockSpec(memory_space=pltpu.VMEM),
        scratch_shapes=[
            pltpu.VMEM(far.shape, jnp.bfloat16),
            pltpu.VMEM(near.shape, jnp.bfloat16),
            pltpu.VMEM((model_width, 2 * width), jnp.bfloat16),
            pltpu.VMEM((model_width, width), jnp.bfloat16),
            pltpu.VMEM((members * SLOT, model_width), jnp.bfloat16),
            pltpu.VMEM((total, COLS), jnp.float32),
        ]
        + [pltpu.SemaphoreType.DMA] * 4,
        compiler_params=pltpu.CompilerParams(vmem_limit_bytes=48 << 20),
        cost_estimate=pl.CostEstimate(
            flops=6 * members * SLOT * model_width * width,
            bytes_accessed=12 << 20,
            transcendentals=members * SLOT * width,
        ),
    )(position, far, near, own, other)


def body(tokens, route_ids, route_gates, gate_up, down_weight):
    model_width = tokens.shape[1]
    dp = lax.axis_index("dp")
    core = dp % 2

    shard = jnp.concatenate((gate_up, down_weight.T[None]), axis=0)
    half = shard.shape[1] // 2
    kept = lax.dynamic_slice_in_dim(shard, core * half, half, axis=1)
    given = lax.dynamic_slice_in_dim(shard, (1 - core) * half, half, axis=1)
    weights = jnp.stack((kept, swap_cores(given)))

    matches = route_ids == 0
    routed = jnp.any(matches, axis=1)
    weight = jnp.sum(jnp.where(matches, route_gates, 0.0), axis=1)
    places = jnp.cumsum(routed.astype(jnp.int32)) - 1
    capacity_ids = jnp.arange(CAP, dtype=jnp.int32)
    packing = (routed[None, :] & (places[None, :] == capacity_ids[:, None])).astype(jnp.bfloat16)
    packed = jnp.dot(packing, tokens, preferred_element_type=jnp.float32).astype(jnp.bfloat16)
    packed = jnp.concatenate((packed[:, : model_width // 2], packed[:, model_width // 2 :]), axis=0)
    far, weights = lax.optimization_barrier((packed[:, :FAR], weights))
    far = lax.all_gather(far, "expert", axis=0, tiled=True)

    weights = jnp.stack([weights] + [turn_plane(weights, s, False) for s in STEPS[1:]])
    near, weights = lax.optimization_barrier((packed[:, FAR:], weights))
    near = lax.all_gather(near, "expert", axis=0, tiled=True)
    own = jnp.stack([weights] + [turn_plane(weights, s, True) for s in STEPS[1:]])
    other = swap_cores(own)

    position = jnp.stack((dp // 8, dp // 2 % 4, core)).astype(jnp.int32)
    partial_value = ffn(position, far, near, own, other)
    summed = lax.psum_scatter(partial_value, "expert", scatter_dimension=0, tiled=True)
    summed = lax.optimization_barrier(summed)
    blocks = model_width // COLS
    summed = summed[: blocks * CAP].reshape(blocks, CAP, COLS)
    summed = jnp.transpose(summed, (1, 0, 2)).reshape(CAP, model_width)
    selector = routed[:, None] & (places[:, None] == capacity_ids[None, :])
    scaled = jnp.where(selector, weight[:, None], 0.0)
    mixed = jnp.dot(
        scaled,
        summed.astype(jnp.float32),
        precision=lax.Precision.HIGHEST,
        preferred_element_type=jnp.float32,
    )
    return mixed.astype(jnp.bfloat16)


def solution(mesh):
    return jax.shard_map(
        body,
        mesh=mesh,
        in_specs=(
            P(("dp", "expert"), None),
            P(("dp", "expert"), None),
            P(("dp", "expert"), None),
            P(None, "dp", "expert"),
            P("expert", "dp"),
        ),
        out_specs=P(("dp", "expert"), None),
        check_vma=False,
    )
```

```python
import functools

import jax
import jax.numpy as jnp
from jax import lax
from jax.experimental import pallas as pl
from jax.experimental.pallas import tpu as pltpu
from jax.sharding import PartitionSpec as P


CAP = 12
SLOT = 16
COLS = 1024
STEPS = (0, 1, 3, 2)


def swap_cores(block):
    return lax.ppermute(block, "dp", [(i, i ^ 1) for i in range(32)])


def turn_plane(block, step, flip):
    routes = []
    for x in range(4):
        for y in range(4):
            for core in range(2):
                along_x = (core == 0) != flip
                source = ((x + step) % 4, y) if along_x else (x, (y + step) % 4)
                routes.append((source[0] * 8 + source[1] * 2 + core, x * 8 + y * 2 + core))
    return lax.ppermute(block, "dp", routes)


def turn_column(block, step, members):
    return lax.ppermute(block, "expert", [(i, (i + step) % members) for i in range(members)])


def ffn_kernel(pos_ref, *refs):
    token_refs, refs = refs[:-10], refs[-10:]
    own_ref, other_ref, out_ref, weights, tokens, rows, sums, total, token_sem, weight_sem = refs
    model_width, hidden_width = weights.shape[0], weights.shape[1] // 3
    members = tokens.shape[0]
    depth = own_ref.shape[2]
    half_width = model_width // 2
    x, y, core, z = pos_ref[0], pos_ref[1], pos_ref[2], pos_ref[3]

    around = members // 2
    steps = [0]
    for k in range(1, around):
        steps += [members - k, k]
    for block, step in zip(token_refs[:-2], steps, strict=True):
        plane = (z + step) & (members - 1)
        pltpu.make_async_copy(block, tokens.at[plane], token_sem).start()
    plane = (z + around) & (members - 1)
    quarter = half_width // 2
    for i, block in enumerate(token_refs[-2:]):
        pltpu.make_async_copy(
            block, tokens.at[plane, :, i * quarter : (i + 1) * quarter], token_sem
        ).start()
    for source, holder in ((own_ref, core), (other_ref, 1 - core)):
        for k, outer in enumerate(STEPS):
            for i, inner in enumerate(STEPS):
                dx = inner + holder * (outer - inner)
                dy = outer + holder * (inner - outer)
                place = ((x + dx) & 3) * 8 + ((y + dy) & 3) * 2 + holder
                start = pl.multiple_of(place * depth, 16)
                pltpu.make_async_copy(
                    source.at[k, i], weights.at[pl.ds(start, depth), :], weight_sem
                ).start()
    pltpu.make_async_copy(tokens, tokens, token_sem).wait()
    for s in range(members):
        for h in range(2):
            rows[s * SLOT : s * SLOT + CAP, h * half_width : (h + 1) * half_width] = tokens[
                s, h * CAP : (h + 1) * CAP, :
            ]
    pltpu.make_async_copy(weights, weights, weight_sem).wait()

    chunk = 1024
    wide = 2 * hidden_width
    both = jnp.zeros((members * SLOT, wide), jnp.float32)
    for j in range(model_width // chunk):
        part = slice(j * chunk, (j + 1) * chunk)
        both += jnp.dot(rows[:, part], weights[part, :wide], preferred_element_type=jnp.float32)
    gate, up = both[:, :hidden_width], both[:, hidden_width:]
    hidden = (gate / (1.0 + jnp.exp(-gate)) * up).astype(jnp.bfloat16)
    stride = sums.shape[0] // members
    blocks = model_width // COLS
    for j in range(blocks):
        result = lax.dot_general(
            hidden,
            weights[j * COLS : (j + 1) * COLS, wide:],
            (((1,), (1,)), ((), ())),
            preferred_element_type=jnp.float32,
        )
        for s in range(members):
            first = s * stride + j * CAP
            sums[first : first + CAP, :] = result[s * SLOT : s * SLOT + CAP, :]
    for s in range(members):
        sums[s * stride + blocks * CAP : (s + 1) * stride, :] = jnp.zeros(
            (stride - blocks * CAP, COLS), jnp.float32
        )
    for r in range(0, sums.shape[0], 464):
        for q in range(r, r + 464, 16):
            total[q : q + 16, :] = sums[q : q + 16, :].astype(jnp.bfloat16)
        part = pl.ds(r, 464)
        pltpu.make_async_copy(total.at[part], out_ref.at[part], weight_sem).start()
    pltpu.make_async_copy(total, out_ref, weight_sem).wait()


def ffn(position, blocks, own, other, members, model_width):
    used = model_width // COLS * CAP
    stride = used // 8 * 8 + 7
    total = members * stride
    anywhere = pl.BlockSpec(memory_space=pl.ANY)
    return pl.pallas_call(
        ffn_kernel,
        out_shape=jax.ShapeDtypeStruct((total, COLS), jnp.bfloat16),
        in_specs=[pl.BlockSpec(memory_space=pltpu.SMEM)] + [anywhere] * (len(blocks) + 2),
        out_specs=pl.BlockSpec(memory_space=pltpu.HBM),
        scratch_shapes=[
            pltpu.VMEM((model_width, own.shape[-1]), jnp.bfloat16),
            pltpu.VMEM((members, 2 * CAP, model_width // 2), jnp.bfloat16),
            pltpu.VMEM((members * SLOT, model_width), jnp.bfloat16),
            pltpu.VMEM((total, COLS), jnp.float32),
            pltpu.VMEM((total, COLS), jnp.bfloat16),
            pltpu.SemaphoreType.DMA,
            pltpu.SemaphoreType.DMA,
        ],
        compiler_params=pltpu.CompilerParams(vmem_limit_bytes=60 << 20),
        cost_estimate=pl.CostEstimate(
            flops=2 * members * SLOT * model_width * own.shape[-1],
            bytes_accessed=14 << 20,
            transcendentals=members * SLOT * own.shape[-1] // 3,
        ),
    )(position, *blocks, own, other)


def body(tokens, route_ids, route_gates, gate_up, down_weight):
    members = lax.axis_size("expert")
    model_width = tokens.shape[1]
    dp, z = lax.axis_index("dp"), lax.axis_index("expert")

    shard = jnp.concatenate((gate_up[0], gate_up[1], down_weight.T), axis=1)
    pieces = [shard, turn_plane(shard, STEPS[1], False)]

    matches = route_ids == 0
    routed = jnp.any(matches, axis=1)
    weight = jnp.sum(jnp.where(matches, route_gates, 0.0), axis=1)
    places = jnp.cumsum(routed.astype(jnp.int32)) - 1
    capacity_ids = jnp.arange(CAP, dtype=jnp.int32)
    packing = (routed[None, :] & (places[None, :] == capacity_ids[:, None])).astype(jnp.bfloat16)
    packed = jnp.dot(packing, tokens, preferred_element_type=jnp.float32).astype(jnp.bfloat16)
    packed = jnp.concatenate((packed[:, : model_width // 2], packed[:, model_width // 2 :]), axis=0)

    blocks = [packed]
    ahead = behind = packed
    own = other = None
    around = members // 2
    for k in range(1, around + 1):
        if k in (2, 3):
            ready, ahead, behind = lax.optimization_barrier((shard, ahead, behind))
            pieces.append(turn_plane(ready, STEPS[k], False))
        elif k in (4, 5, 6):
            if k == 4:
                bundle = jnp.stack(pieces)
                pieces = [bundle]
            ready, ahead, behind = lax.optimization_barrier((bundle, ahead, behind))
            pieces.append(turn_plane(ready, STEPS[(3, 1, 2)[k - 4]], True))
        elif k == around:
            own = jnp.stack((pieces[0], pieces[2], pieces[3], pieces[1]))
            ready, ahead, behind = lax.optimization_barrier((own, ahead, behind))
            other = swap_cores(ready)
            ahead, behind = ahead[:, : model_width // 4], behind[:, model_width // 4 :]
        else:
            ahead, behind = lax.optimization_barrier((ahead, behind))
        ahead = turn_column(ahead, 1, members)
        behind = turn_column(behind, -1, members)
        blocks += [ahead, behind]

    position = jnp.stack((dp // 8, dp // 2 % 4, dp % 2, z)).astype(jnp.int32)
    partial_value = ffn(position, blocks, own, other, members, model_width)
    summed = lax.psum_scatter(partial_value, "expert", scatter_dimension=0, tiled=True)
    summed = lax.optimization_barrier(summed)
    blocks = model_width // COLS
    summed = summed[: blocks * CAP].reshape(blocks, CAP, COLS)
    summed = jnp.transpose(summed, (1, 0, 2)).reshape(CAP, model_width)
    selector = routed[:, None] & (places[:, None] == capacity_ids[None, :])
    scaled = jnp.where(selector, weight[:, None], 0.0)
    mixed = jnp.dot(
        scaled,
        summed.astype(jnp.float32),
        precision=lax.Precision.HIGHEST,
        preferred_element_type=jnp.float32,
    )
    return mixed.astype(jnp.bfloat16)


def solution(mesh):
    return jax.shard_map(
        body,
        mesh=mesh,
        in_specs=(
            P(("dp", "expert"), None),
            P(("dp", "expert"), None),
            P(("dp", "expert"), None),
            P(None, "dp", "expert"),
            P("expert", "dp"),
        ),
        out_specs=P(("dp", "expert"), None),
        check_vma=False,
    )
```

```python
import functools

import jax
import jax.numpy as jnp
from jax import lax
from jax.experimental import pallas as pl
from jax.experimental.pallas import tpu as pltpu
from jax.sharding import PartitionSpec as P


CAP = 12
SLOT = 16
COLS = 1024
STEPS = (0, 1, 3, 2)


def swap_cores(block):
    return lax.ppermute(block, "dp", [(i, i ^ 1) for i in range(32)])


def turn_plane(block, step, flip):
    routes = []
    for x in range(4):
        for y in range(4):
            for core in range(2):
                along_x = (core == 0) != flip
                source = ((x + step) % 4, y) if along_x else (x, (y + step) % 4)
                routes.append((source[0] * 8 + source[1] * 2 + core, x * 8 + y * 2 + core))
    return lax.ppermute(block, "dp", routes)


def place_kernel(pos_ref, own_ref, other_ref, out_ref, weights, sem):
    depth = own_ref.shape[2]
    x, y, core = pos_ref[0], pos_ref[1], pos_ref[2]
    for source, holder in ((own_ref, core), (other_ref, 1 - core)):
        for k, outer in enumerate(STEPS):
            for i, inner in enumerate(STEPS):
                dx = inner + holder * (outer - inner)
                dy = outer + holder * (inner - outer)
                place = ((x + dx) & 3) * 8 + ((y + dy) & 3) * 2 + holder
                start = pl.multiple_of(place * depth, 16)
                pltpu.make_async_copy(
                    source.at[k, i], weights.at[pl.ds(start, depth), :], sem
                ).start()
    pltpu.make_async_copy(weights, weights, sem).wait()
    pltpu.make_async_copy(weights, out_ref, sem).start()
    pltpu.make_async_copy(weights, out_ref, sem).wait()


def place_weights(position, own, other, model_width):
    anywhere = pl.BlockSpec(memory_space=pl.ANY)
    shape = (model_width, own.shape[-1])
    return pl.pallas_call(
        place_kernel,
        out_shape=jax.ShapeDtypeStruct(shape, jnp.bfloat16),
        in_specs=[pl.BlockSpec(memory_space=pltpu.SMEM)] + [anywhere] * 2,
        out_specs=anywhere,
        scratch_shapes=[pltpu.VMEM(shape, jnp.bfloat16), pltpu.SemaphoreType.DMA],
        compiler_params=pltpu.CompilerParams(vmem_limit_bytes=60 << 20),
        cost_estimate=pl.CostEstimate(flops=0, bytes_accessed=22 << 20, transcendentals=0),
    )(position, own, other)


def ffn_kernel(tokens_ref, weights_ref, out_ref, tokens, weights, rows, sums, total, sem, piece_sem):
    model_width, hidden_width = weights.shape[0], weights.shape[1] // 3
    members = tokens.shape[0] // (2 * CAP)
    half_width = model_width // 2
    wide = 2 * hidden_width
    pieces = piece_sem.shape[0]
    piece = model_width // pieces

    def fetch(j):
        part = pl.ds(j * piece, piece)
        return pltpu.make_async_copy(weights_ref.at[part], weights.at[part], piece_sem.at[j])

    pltpu.make_async_copy(tokens_ref, tokens, sem).start()
    for j in range(pieces):
        fetch(j).start()
    pltpu.make_async_copy(tokens_ref, tokens, sem).wait()
    both = jnp.zeros((members * SLOT, wide), jnp.float32)
    for j in range(pieces):
        for first in (j * piece, j * piece + piece // 2):
            h, offset = divmod(first, half_width)
            for s in range(members):
                rows[s * SLOT : s * SLOT + CAP, first : first + piece // 2] = tokens[
                    (2 * s + h) * CAP : (2 * s + h + 1) * CAP, offset : offset + piece // 2
                ]
        fetch(j).wait()
        part = slice(j * piece, (j + 1) * piece)
        both += jnp.dot(rows[:, part], weights[part, :wide], preferred_element_type=jnp.float32)
    gate, up = both[:, :hidden_width], both[:, hidden_width:]
    hidden = (gate / (1.0 + jnp.exp(-gate)) * up).astype(jnp.bfloat16)
    stride = sums.shape[0] // members
    blocks = model_width // COLS
    for j in range(blocks):
        result = lax.dot_general(
            hidden,
            weights[j * COLS : (j + 1) * COLS, wide:],
            (((1,), (1,)), ((), ())),
            preferred_element_type=jnp.float32,
        )
        for s in range(members):
            first = s * stride + j * CAP
            sums[first : first + CAP, :] = result[s * SLOT : s * SLOT + CAP, :]
    for s in range(members):
        sums[s * stride + blocks * CAP : (s + 1) * stride, :] = jnp.zeros(
            (stride - blocks * CAP, COLS), jnp.float32
        )
    for r in range(0, sums.shape[0], 464):
        for q in range(r, r + 464, 16):
            total[q : q + 16, :] = sums[q : q + 16, :].astype(jnp.bfloat16)
        part = pl.ds(r, 464)
        pltpu.make_async_copy(total.at[part], out_ref.at[part], sem).start()
    pltpu.make_async_copy(total, out_ref, sem).wait()


def ffn(gathered, weights):
    model_width, width = weights.shape
    members = gathered.shape[0] // (2 * CAP)
    used = model_width // COLS * CAP
    stride = used // 8 * 8 + 7
    total = members * stride
    anywhere = pl.BlockSpec(memory_space=pl.ANY)
    return pl.pallas_call(
        ffn_kernel,
        out_shape=jax.ShapeDtypeStruct((total, COLS), jnp.bfloat16),
        in_specs=[anywhere] * 2,
        out_specs=anywhere,
        scratch_shapes=[
            pltpu.VMEM(gathered.shape, jnp.bfloat16),
            pltpu.VMEM(weights.shape, jnp.bfloat16),
            pltpu.VMEM((members * SLOT, model_width), jnp.bfloat16),
            pltpu.VMEM((total, COLS), jnp.float32),
            pltpu.VMEM((total, COLS), jnp.bfloat16),
            pltpu.SemaphoreType.DMA,
            pltpu.SemaphoreType.DMA((7,)),
        ],
        compiler_params=pltpu.CompilerParams(vmem_limit_bytes=60 << 20),
        cost_estimate=pl.CostEstimate(
            flops=2 * members * SLOT * model_width * width,
            bytes_accessed=14 << 20,
            transcendentals=members * SLOT * width // 3,
        ),
    )(gathered, weights)


def body(tokens, route_ids, route_gates, gate_up, down_weight):
    model_width = tokens.shape[1]
    dp = lax.axis_index("dp")

    matches = route_ids == 0
    routed = jnp.any(matches, axis=1)
    weight = jnp.sum(jnp.where(matches, route_gates, 0.0), axis=1)
    places = jnp.cumsum(routed.astype(jnp.int32)) - 1
    capacity_ids = jnp.arange(CAP, dtype=jnp.int32)
    packing = (routed[None, :] & (places[None, :] == capacity_ids[:, None])).astype(jnp.bfloat16)
    packed = jnp.dot(packing, tokens, preferred_element_type=jnp.float32).astype(jnp.bfloat16)
    packed = jnp.concatenate((packed[:, : model_width // 2], packed[:, model_width // 2 :]), axis=0)

    shard = jnp.concatenate((gate_up[0], gate_up[1], down_weight.T), axis=1)
    packed, shard = lax.optimization_barrier((packed, shard))
    gathered = lax.all_gather(packed, "expert", axis=0, tiled=True)
    bundle = jnp.stack([shard] + [turn_plane(shard, s, False) for s in STEPS[1:]])
    own = jnp.stack([bundle] + [turn_plane(bundle, s, True) for s in STEPS[1:]])
    other = swap_cores(own)
    position = jnp.stack((dp // 8, dp // 2 % 4, dp % 2)).astype(jnp.int32)
    weights = place_weights(position, own, other, model_width)
    partial_value = ffn(gathered, weights)
    summed = lax.psum_scatter(partial_value, "expert", scatter_dimension=0, tiled=True)
    summed = lax.optimization_barrier(summed)
    blocks = model_width // COLS
    summed = summed[: blocks * CAP].reshape(blocks, CAP, COLS)
    summed = jnp.transpose(summed, (1, 0, 2)).reshape(CAP, model_width)
    selector = routed[:, None] & (places[:, None] == capacity_ids[None, :])
    scaled = jnp.where(selector, weight[:, None], 0.0)
    mixed = jnp.dot(
        scaled,
        summed.astype(jnp.float32),
        precision=lax.Precision.HIGHEST,
        preferred_element_type=jnp.float32,
    )
    return mixed.astype(jnp.bfloat16)


def solution(mesh):
    return jax.shard_map(
        body,
        mesh=mesh,
        in_specs=(
            P(("dp", "expert"), None),
            P(("dp", "expert"), None),
            P(("dp", "expert"), None),
            P(None, "dp", "expert"),
            P("expert", "dp"),
        ),
        out_specs=P(("dp", "expert"), None),
        check_vma=False,
    )
```

```python
import functools

import jax
import jax.numpy as jnp
from jax import lax
from jax.experimental import pallas as pl
from jax.experimental.pallas import tpu as pltpu
from jax.sharding import PartitionSpec as P


CAP = 12
COLS = 1024
STEPS = (0, 1, 3, 2)


def swap_cores(block):
    return lax.ppermute(block, "dp", [(i, i ^ 1) for i in range(32)])


def turn_plane(block, step, flip):
    routes = []
    for x in range(4):
        for y in range(4):
            for core in range(2):
                along_x = (core == 0) != flip
                source = ((x + step) % 4, y) if along_x else (x, (y + step) % 4)
                routes.append((source[0] * 8 + source[1] * 2 + core, x * 8 + y * 2 + core))
    return lax.ppermute(block, "dp", routes)


def place_kernel(pos_ref, own_ref, other_ref, out_ref, weights, sem):
    depth = own_ref.shape[2]
    x, y, core = pos_ref[0], pos_ref[1], pos_ref[2]
    for source, holder in ((own_ref, core), (other_ref, 1 - core)):
        for k, outer in enumerate(STEPS):
            for i, inner in enumerate(STEPS):
                dx = inner + holder * (outer - inner)
                dy = outer + holder * (inner - outer)
                place = ((x + dx) & 3) * 8 + ((y + dy) & 3) * 2 + holder
                start = pl.multiple_of(place * depth, 16)
                pltpu.make_async_copy(
                    source.at[k, i], weights.at[pl.ds(start, depth), :], sem
                ).start()
    pltpu.make_async_copy(weights, weights, sem).wait()
    pltpu.make_async_copy(weights, out_ref, sem).start()
    pltpu.make_async_copy(weights, out_ref, sem).wait()


def place_weights(position, own, other, model_width):
    anywhere = pl.BlockSpec(memory_space=pl.ANY)
    shape = (model_width, own.shape[-1])
    return pl.pallas_call(
        place_kernel,
        out_shape=jax.ShapeDtypeStruct(shape, jnp.bfloat16),
        in_specs=[pl.BlockSpec(memory_space=pltpu.SMEM)] + [anywhere] * 2,
        out_specs=anywhere,
        scratch_shapes=[pltpu.VMEM(shape, jnp.bfloat16), pltpu.SemaphoreType.DMA],
        compiler_params=pltpu.CompilerParams(vmem_limit_bytes=60 << 20),
        cost_estimate=pl.CostEstimate(flops=0, bytes_accessed=22 << 20, transcendentals=0),
    )(position, own, other)


def route(ids_ref, gates_ref):
    count = ids_ref.shape[1]
    matches = ids_ref[...] == 0
    routed = jnp.max(matches.astype(jnp.float32), axis=0, keepdims=True)
    weight = jnp.sum(jnp.where(matches, gates_ref[...], 0.0), axis=0, keepdims=True)
    earlier = lax.broadcasted_iota(jnp.int32, (count, count), 0)
    later = lax.broadcasted_iota(jnp.int32, (count, count), 1)
    upto = (earlier <= later).astype(jnp.bfloat16)
    counts = jnp.dot(
        jnp.broadcast_to(routed, (8, count)).astype(jnp.bfloat16),
        upto,
        preferred_element_type=jnp.float32,
    )[:1]
    place = jnp.where(routed > 0.0, counts - 1.0, -1.0).astype(jnp.int32)
    return weight, place


def pack_kernel(ids_ref, gates_ref, tokens_ref, packed_ref):
    _, place = route(ids_ref, gates_ref)
    half_width = packed_ref.shape[1]
    slot = lax.broadcasted_iota(jnp.int32, (2 * CAP, place.shape[1]), 0)
    first = ((slot == place) & (slot < CAP)).astype(jnp.float32).astype(jnp.bfloat16)
    second = ((slot == place + CAP) & (slot >= CAP) & (place >= 0)).astype(jnp.float32).astype(jnp.bfloat16)
    packed_ref[...] = (
        jnp.dot(first, tokens_ref[:, :half_width], preferred_element_type=jnp.float32)
        + jnp.dot(second, tokens_ref[:, half_width:], preferred_element_type=jnp.float32)
    ).astype(jnp.bfloat16)


def pack(ids, gates, tokens):
    count, model_width = tokens.shape
    vmem = pl.BlockSpec(memory_space=pltpu.VMEM)
    return pl.pallas_call(
        pack_kernel,
        out_shape=jax.ShapeDtypeStruct((2 * CAP, model_width // 2), jnp.bfloat16),
        in_specs=[vmem] * 3,
        out_specs=vmem,
        cost_estimate=pl.CostEstimate(
            flops=4 * CAP * count * model_width, bytes_accessed=2 << 20, transcendentals=0
        ),
    )(ids, gates, tokens)


def mix_kernel(ids_ref, gates_ref, summed_ref, out_ref, padded):
    weight, place = route(ids_ref, gates_ref)
    count = place.shape[1]
    weight = jnp.transpose(jnp.broadcast_to(weight, (count, count)))[:, :1]
    place = jnp.transpose(jnp.broadcast_to(place, (count, count)))
    depth = summed_ref.shape[0]
    padded[depth // 16 * 16 :, :] = jnp.zeros((count - depth // 16 * 16, COLS), jnp.bfloat16)
    padded[:depth, :] = summed_ref[...]
    slot = lax.broadcasted_iota(jnp.int32, (count, count), 1)
    for j in range(out_ref.shape[1] // COLS):
        chosen = (slot == place + j * CAP) & (place >= 0)
        picked = jnp.dot(
            chosen.astype(jnp.float32).astype(jnp.bfloat16),
            padded[...],
            preferred_element_type=jnp.float32,
        )
        out_ref[:, j * COLS : (j + 1) * COLS] = (weight * picked).astype(jnp.bfloat16)


def mix(ids, gates, summed, model_width):
    count = ids.shape[1]
    vmem = pl.BlockSpec(memory_space=pltpu.VMEM)
    return pl.pallas_call(
        mix_kernel,
        out_shape=jax.ShapeDtypeStruct((count, model_width), jnp.bfloat16),
        in_specs=[vmem] * 3,
        out_specs=vmem,
        scratch_shapes=[pltpu.VMEM((count, COLS), jnp.bfloat16)],
        cost_estimate=pl.CostEstimate(
            flops=2 * count * summed.shape[0] * model_width, bytes_accessed=2 << 20, transcendentals=0
        ),
    )(ids, gates, summed)


def ffn_kernel(tokens_ref, weights_ref, out_ref, tokens, weights, rows, sums, total, sem, piece_sem):
    model_width, hidden_width = weights.shape[0], weights.shape[1] // 3
    members = tokens.shape[0] // (2 * CAP)
    half_width = model_width // 2
    wide = 2 * hidden_width
    pieces = piece_sem.shape[0]
    piece = model_width // pieces

    def fetch(j):
        part = pl.ds(j * piece, piece)
        return pltpu.make_async_copy(weights_ref.at[part], weights.at[part], piece_sem.at[j])

    pltpu.make_async_copy(tokens_ref, tokens, sem).start()
    for j in range(pieces):
        fetch(j).start()
    pltpu.make_async_copy(tokens_ref, tokens, sem).wait()
    both = jnp.zeros((members * CAP, wide), jnp.float32)
    for j in range(pieces):
        for first in (j * piece, j * piece + piece // 2):
            h, offset = divmod(first, half_width)
            for s in range(members):
                rows[s * CAP : (s + 1) * CAP, first : first + piece // 2] = tokens[
                    (2 * s + h) * CAP : (2 * s + h + 1) * CAP, offset : offset + piece // 2
                ]
        fetch(j).wait()
        part = slice(j * piece, (j + 1) * piece)
        both += jnp.dot(rows[:, part], weights[part, :wide], preferred_element_type=jnp.float32)
    gate, up = both[:, :hidden_width], both[:, hidden_width:]
    hidden = (gate / (1.0 + jnp.exp(-gate)) * up).astype(jnp.bfloat16)
    stride = sums.shape[0] // members
    blocks = model_width // COLS
    for j in range(blocks):
        result = lax.dot_general(
            hidden,
            weights[j * COLS : (j + 1) * COLS, wide:],
            (((1,), (1,)), ((), ())),
            preferred_element_type=jnp.float32,
        )
        for s in range(members):
            first = s * stride + j * CAP
            sums[first : first + CAP, :] = result[s * CAP : (s + 1) * CAP, :]
    for s in range(members):
        sums[s * stride + blocks * CAP : (s + 1) * stride, :] = jnp.zeros(
            (stride - blocks * CAP, COLS), jnp.float32
        )
    for r in range(0, sums.shape[0], 464):
        for q in range(r, r + 464, 16):
            total[q : q + 16, :] = sums[q : q + 16, :].astype(jnp.bfloat16)
        part = pl.ds(r, 464)
        pltpu.make_async_copy(total.at[part], out_ref.at[part], sem).start()
    pltpu.make_async_copy(total, out_ref, sem).wait()


def ffn(gathered, weights):
    model_width, width = weights.shape
    members = gathered.shape[0] // (2 * CAP)
    used = model_width // COLS * CAP
    stride = used // 8 * 8 + 7
    total = members * stride
    anywhere = pl.BlockSpec(memory_space=pl.ANY)
    return pl.pallas_call(
        ffn_kernel,
        out_shape=jax.ShapeDtypeStruct((total, COLS), jnp.bfloat16),
        in_specs=[anywhere] * 2,
        out_specs=anywhere,
        scratch_shapes=[
            pltpu.VMEM(gathered.shape, jnp.bfloat16),
            pltpu.VMEM(weights.shape, jnp.bfloat16),
            pltpu.VMEM((members * CAP, model_width), jnp.bfloat16),
            pltpu.VMEM((total, COLS), jnp.float32),
            pltpu.VMEM((total, COLS), jnp.bfloat16),
            pltpu.SemaphoreType.DMA,
            pltpu.SemaphoreType.DMA((7,)),
        ],
        compiler_params=pltpu.CompilerParams(vmem_limit_bytes=60 << 20),
        cost_estimate=pl.CostEstimate(
            flops=2 * members * CAP * model_width * width,
            bytes_accessed=14 << 20,
            transcendentals=members * CAP * width // 3,
        ),
    )(gathered, weights)


def body(tokens, route_ids, route_gates, gate_up, down_weight):
    model_width = tokens.shape[1]
    dp = lax.axis_index("dp")

    ids, gates = route_ids.T, route_gates.T
    packed = pack(ids, gates, tokens)

    shard = jnp.concatenate((gate_up[0], gate_up[1], down_weight.T), axis=1)
    packed, shard = lax.optimization_barrier((packed, shard))
    gathered = lax.all_gather(packed, "expert", axis=0, tiled=True)
    bundle = jnp.stack([shard] + [turn_plane(shard, s, False) for s in STEPS[1:]])
    own = jnp.stack([bundle] + [turn_plane(bundle, s, True) for s in STEPS[1:]])
    other = swap_cores(own)
    position = jnp.stack((dp // 8, dp // 2 % 4, dp % 2)).astype(jnp.int32)
    weights = place_weights(position, own, other, model_width)
    partial_value = ffn(gathered, weights)
    summed = lax.psum_scatter(partial_value, "expert", scatter_dimension=0, tiled=True)
    summed = lax.optimization_barrier(summed)
    return mix(ids, gates, summed, model_width)


def solution(mesh):
    return jax.shard_map(
        body,
        mesh=mesh,
        in_specs=(
            P(("dp", "expert"), None),
            P(("dp", "expert"), None),
            P(("dp", "expert"), None),
            P(None, "dp", "expert"),
            P("expert", "dp"),
        ),
        out_specs=P(("dp", "expert"), None),
        check_vma=False,
    )
```

```python
import functools

import jax
import jax.numpy as jnp
from jax import lax
from jax.experimental import pallas as pl
from jax.experimental.pallas import tpu as pltpu
from jax.sharding import PartitionSpec as P


CAP = 12
COLS = 1024
STEPS = (0, 1, 3, 2)


def swap_cores(block):
    return lax.ppermute(block, "dp", [(i, i ^ 1) for i in range(32)])


def turn_plane(block, step, flip):
    routes = []
    for x in range(4):
        for y in range(4):
            for core in range(2):
                along_x = (core == 0) != flip
                source = ((x + step) % 4, y) if along_x else (x, (y + step) % 4)
                routes.append((source[0] * 8 + source[1] * 2 + core, x * 8 + y * 2 + core))
    return lax.ppermute(block, "dp", routes)


def place_kernel(
    pos_ref, own_ref, other_ref, wide_ref, down_ref, weights, turned, sem, wide_sem, down_sem
):
    depth = own_ref.shape[2]
    model_width, wide = wide_ref.shape
    x, y, core = pos_ref[0], pos_ref[1], pos_ref[2]
    for source, holder in ((own_ref, core), (other_ref, 1 - core)):
        for k, outer in enumerate(STEPS):
            for i, inner in enumerate(STEPS):
                dx = inner + holder * (outer - inner)
                dy = outer + holder * (inner - outer)
                place = ((x + dx) & 3) * 8 + ((y + dy) & 3) * 2 + holder
                start = pl.multiple_of(place * depth, 16)
                pltpu.make_async_copy(
                    source.at[k, i], weights.at[pl.ds(start, depth), :], sem
                ).start()
    pltpu.make_async_copy(weights, weights, sem).wait()
    straight = pltpu.make_async_copy(weights.at[:, :wide], wide_ref, wide_sem)
    straight.start()
    for j in range(0, model_width, 512):
        turned[:, j : j + 512] = jnp.transpose(weights[j : j + 512, wide:])
    across = pltpu.make_async_copy(turned, down_ref, down_sem)
    across.start()
    straight.wait()
    across.wait()


def place_weights(position, own, other, model_width):
    anywhere = pl.BlockSpec(memory_space=pl.ANY)
    width = own.shape[-1] // 3
    return pl.pallas_call(
        place_kernel,
        out_shape=(
            jax.ShapeDtypeStruct((model_width, 2 * width), jnp.bfloat16),
            jax.ShapeDtypeStruct((width, model_width), jnp.bfloat16),
        ),
        in_specs=[pl.BlockSpec(memory_space=pltpu.SMEM)] + [anywhere] * 2,
        out_specs=(anywhere, anywhere),
        scratch_shapes=[
            pltpu.VMEM((model_width, 3 * width), jnp.bfloat16),
            pltpu.VMEM((width, model_width), jnp.bfloat16),
        ]
        + [pltpu.SemaphoreType.DMA] * 3,
        compiler_params=pltpu.CompilerParams(vmem_limit_bytes=60 << 20),
        cost_estimate=pl.CostEstimate(flops=0, bytes_accessed=22 << 20, transcendentals=0),
    )(position, own, other)


def ffn_kernel(
    tokens_ref, wide_ref, down_ref, out_ref,
    tokens, wide, down, rows, sums, total, token_sem, wide_sem, down_sem, out_sem,
):
    hidden_width, model_width = down.shape
    members = tokens.shape[0] // (2 * CAP)
    half_width = model_width // 2
    pieces = token_sem.shape[0]
    piece = half_width // pieces

    def fetch_tokens(o):
        part = (slice(None), slice(o * piece, (o + 1) * piece))
        return pltpu.make_async_copy(tokens_ref.at[part], tokens.at[part], token_sem.at[o])

    def fetch_wide(o, h):
        part = pl.ds(h * half_width + o * piece, piece)
        return pltpu.make_async_copy(wide_ref.at[part], wide.at[part], wide_sem.at[2 * o + h])

    for o in range(pieces):
        fetch_tokens(o).start()
        fetch_wide(o, 0).start()
        fetch_wide(o, 1).start()
    whole_down = pltpu.make_async_copy(down_ref, down, down_sem)
    whole_down.start()
    both = jnp.zeros((members * CAP, 2 * hidden_width), jnp.float32)
    for o in range(pieces):
        fetch_tokens(o).wait()
        for h in range(2):
            part = slice(h * half_width + o * piece, h * half_width + (o + 1) * piece)
            for s in range(members):
                rows[s * CAP : (s + 1) * CAP, part] = tokens[
                    (2 * s + h) * CAP : (2 * s + h + 1) * CAP, o * piece : (o + 1) * piece
                ]
            fetch_wide(o, h).wait()
            both += jnp.dot(rows[:, part], wide[part, :], preferred_element_type=jnp.float32)
    gate, up = both[:, :hidden_width], both[:, hidden_width:]
    hidden = (gate / (1.0 + jnp.exp(-gate)) * up).astype(jnp.bfloat16)
    whole_down.wait()
    stride = sums.shape[0] // members
    blocks = model_width // COLS
    for j in range(blocks):
        result = jnp.dot(
            hidden, down[:, j * COLS : (j + 1) * COLS], preferred_element_type=jnp.float32
        )
        for s in range(members):
            first = s * stride + j * CAP
            sums[first : first + CAP, :] = result[s * CAP : (s + 1) * CAP, :]
    for s in range(members):
        sums[s * stride + blocks * CAP : (s + 1) * stride, :] = jnp.zeros(
            (stride - blocks * CAP, COLS), jnp.float32
        )
    for r in range(0, sums.shape[0], 464):
        for q in range(r, r + 464, 16):
            total[q : q + 16, :] = sums[q : q + 16, :].astype(jnp.bfloat16)
        part = pl.ds(r, 464)
        pltpu.make_async_copy(total.at[part], out_ref.at[part], out_sem).start()
    pltpu.make_async_copy(total, out_ref, out_sem).wait()


def ffn(gathered, wide, down):
    width, model_width = down.shape
    members = gathered.shape[0] // (2 * CAP)
    used = model_width // COLS * CAP
    stride = used // 8 * 8 + 7
    total = members * stride
    anywhere = pl.BlockSpec(memory_space=pl.ANY)
    return pl.pallas_call(
        ffn_kernel,
        out_shape=jax.ShapeDtypeStruct((total, COLS), jnp.bfloat16),
        in_specs=[anywhere] * 3,
        out_specs=anywhere,
        scratch_shapes=[
            pltpu.VMEM(gathered.shape, jnp.bfloat16),
            pltpu.VMEM(wide.shape, jnp.bfloat16),
            pltpu.VMEM(down.shape, jnp.bfloat16),
            pltpu.VMEM((members * CAP, model_width), jnp.bfloat16),
            pltpu.VMEM((total, COLS), jnp.float32),
            pltpu.VMEM((total, COLS), jnp.bfloat16),
            pltpu.SemaphoreType.DMA((7,)),
            pltpu.SemaphoreType.DMA((14,)),
            pltpu.SemaphoreType.DMA,
            pltpu.SemaphoreType.DMA,
        ],
        compiler_params=pltpu.CompilerParams(vmem_limit_bytes=60 << 20),
        cost_estimate=pl.CostEstimate(
            flops=6 * members * CAP * model_width * width,
            bytes_accessed=14 << 20,
            transcendentals=members * CAP * width,
        ),
    )(gathered, wide, down)


def body(tokens, route_ids, route_gates, gate_up, down_weight):
    model_width = tokens.shape[1]
    dp = lax.axis_index("dp")

    matches = route_ids == 0
    routed = jnp.any(matches, axis=1)
    weight = jnp.sum(jnp.where(matches, route_gates, 0.0), axis=1)
    places = jnp.cumsum(routed.astype(jnp.int32)) - 1
    capacity_ids = jnp.arange(CAP, dtype=jnp.int32)
    packing = (routed[None, :] & (places[None, :] == capacity_ids[:, None])).astype(jnp.bfloat16)
    packed = jnp.dot(packing, tokens, preferred_element_type=jnp.float32).astype(jnp.bfloat16)
    packed = jnp.concatenate((packed[:, : model_width // 2], packed[:, model_width // 2 :]), axis=0)

    shard = jnp.concatenate((gate_up[0], gate_up[1], down_weight.T), axis=1)
    packed, shard = lax.optimization_barrier((packed, shard))
    gathered = lax.all_gather(packed, "expert", axis=0, tiled=True)
    bundle = jnp.stack([shard] + [turn_plane(shard, s, False) for s in STEPS[1:]])
    own = jnp.stack([bundle] + [turn_plane(bundle, s, True) for s in STEPS[1:]])
    other = swap_cores(own)
    position = jnp.stack((dp // 8, dp // 2 % 4, dp % 2)).astype(jnp.int32)
    wide, down = place_weights(position, own, other, model_width)
    partial_value = ffn(gathered, wide, down)
    summed = lax.psum_scatter(partial_value, "expert", scatter_dimension=0, tiled=True)
    summed = lax.optimization_barrier(summed)
    blocks = model_width // COLS
    summed = summed[: blocks * CAP].reshape(blocks, CAP, COLS)
    summed = jnp.transpose(summed, (1, 0, 2)).reshape(CAP, model_width)
    selector = routed[:, None] & (places[:, None] == capacity_ids[None, :])
    scaled = jnp.where(selector, weight[:, None], 0.0)
    mixed = jnp.dot(
        scaled,
        summed.astype(jnp.float32),
        precision=lax.Precision.HIGHEST,
        preferred_element_type=jnp.float32,
    )
    return mixed.astype(jnp.bfloat16)


def solution(mesh):
    return jax.shard_map(
        body,
        mesh=mesh,
        in_specs=(
            P(("dp", "expert"), None),
            P(("dp", "expert"), None),
            P(("dp", "expert"), None),
            P(None, "dp", "expert"),
            P("expert", "dp"),
        ),
        out_specs=P(("dp", "expert"), None),
        check_vma=False,
    )
```

```python
import functools

import jax
import jax.numpy as jnp
from jax import lax
from jax.experimental import pallas as pl
from jax.experimental.pallas import tpu as pltpu
from jax.sharding import PartitionSpec as P


CAP = 12
COLS = 256
STEPS = (0, 1, 3, 2)


def swap_cores(block):
    return lax.ppermute(block, "dp", [(i, i ^ 1) for i in range(32)])


def turn_plane(block, step, flip):
    routes = []
    for x in range(4):
        for y in range(4):
            for core in range(2):
                along_x = (core == 0) != flip
                source = ((x + step) % 4, y) if along_x else (x, (y + step) % 4)
                routes.append((source[0] * 8 + source[1] * 2 + core, x * 8 + y * 2 + core))
    return lax.ppermute(block, "dp", routes)


def place_kernel(
    pos_ref, own_ref, other_ref, wide_ref, down_ref, weights, turned, sem, wide_sem, down_sem
):
    depth = own_ref.shape[2]
    model_width, wide = wide_ref.shape
    x, y, core = pos_ref[0], pos_ref[1], pos_ref[2]
    for source, holder in ((own_ref, core), (other_ref, 1 - core)):
        for k, outer in enumerate(STEPS):
            for i, inner in enumerate(STEPS):
                dx = inner + holder * (outer - inner)
                dy = outer + holder * (inner - outer)
                place = ((x + dx) & 3) * 8 + ((y + dy) & 3) * 2 + holder
                start = pl.multiple_of(place * depth, 16)
                pltpu.make_async_copy(
                    source.at[k, i], weights.at[pl.ds(start, depth), :], sem
                ).start()
    pltpu.make_async_copy(weights, weights, sem).wait()
    straight = pltpu.make_async_copy(weights.at[:, :wide], wide_ref, wide_sem)
    straight.start()
    for j in range(0, model_width, 512):
        turned[:, j : j + 512] = jnp.transpose(weights[j : j + 512, wide:])
    across = pltpu.make_async_copy(turned, down_ref, down_sem)
    across.start()
    straight.wait()
    across.wait()


def place_weights(position, own, other, model_width):
    anywhere = pl.BlockSpec(memory_space=pl.ANY)
    width = own.shape[-1] // 3
    return pl.pallas_call(
        place_kernel,
        out_shape=(
            jax.ShapeDtypeStruct((model_width, 2 * width), jnp.bfloat16),
            jax.ShapeDtypeStruct((width, model_width), jnp.bfloat16),
        ),
        in_specs=[pl.BlockSpec(memory_space=pltpu.SMEM)] + [anywhere] * 2,
        out_specs=(anywhere, anywhere),
        scratch_shapes=[
            pltpu.VMEM((model_width, 3 * width), jnp.bfloat16),
            pltpu.VMEM((width, model_width), jnp.bfloat16),
        ]
        + [pltpu.SemaphoreType.DMA] * 3,
        compiler_params=pltpu.CompilerParams(vmem_limit_bytes=60 << 20),
        cost_estimate=pl.CostEstimate(flops=0, bytes_accessed=22 << 20, transcendentals=0),
    )(position, own, other)


def ffn_kernel(
    tokens_ref, wide_ref, down_ref, out_ref,
    tokens, wide, down, rows, sums, total, token_sem, wide_sem, down_sem, out_sem,
):
    hidden_width, model_width = down.shape
    members = tokens.shape[0] // (2 * CAP)
    half_width = model_width // 2
    pieces = token_sem.shape[0]
    piece = half_width // pieces

    def fetch_tokens(o):
        part = (slice(None), slice(o * piece, (o + 1) * piece))
        return pltpu.make_async_copy(tokens_ref.at[part], tokens.at[part], token_sem.at[o])

    def fetch_wide(o, h):
        part = pl.ds(h * half_width + o * piece, piece)
        return pltpu.make_async_copy(wide_ref.at[part], wide.at[part], wide_sem.at[2 * o + h])

    for o in range(pieces):
        fetch_tokens(o).start()
        fetch_wide(o, 0).start()
        fetch_wide(o, 1).start()
    whole_down = pltpu.make_async_copy(down_ref, down, down_sem)
    whole_down.start()
    both = jnp.zeros((members * CAP, 2 * hidden_width), jnp.float32)
    for o in range(pieces):
        fetch_tokens(o).wait()
        for h in range(2):
            part = slice(h * half_width + o * piece, h * half_width + (o + 1) * piece)
            for s in range(members):
                rows[s * CAP : (s + 1) * CAP, part] = tokens[
                    (2 * s + h) * CAP : (2 * s + h + 1) * CAP, o * piece : (o + 1) * piece
                ]
            fetch_wide(o, h).wait()
            both += jnp.dot(rows[:, part], wide[part, :], preferred_element_type=jnp.float32)
    gate, up = both[:, :hidden_width], both[:, hidden_width:]
    hidden = (gate / (1.0 + jnp.exp(-gate)) * up).astype(jnp.bfloat16)
    whole_down.wait()
    stride = sums.shape[0] // members
    blocks = model_width // COLS
    group = 4
    for j in range(0, blocks, group):
        result = jnp.dot(
            hidden, down[:, j * COLS : (j + group) * COLS], preferred_element_type=jnp.float32
        )
        for s in range(members):
            for q in range(group):
                first = s * stride + (j + q) * CAP
                sums[first : first + CAP, :] = result[
                    s * CAP : (s + 1) * CAP, q * COLS : (q + 1) * COLS
                ]
    for s in range(members):
        sums[s * stride + blocks * CAP : (s + 1) * stride, :] = jnp.zeros(
            (stride - blocks * CAP, COLS), jnp.float32
        )
    for r in range(0, sums.shape[0], 784):
        for q in range(r, r + 784, 16):
            total[q : q + 16, :] = sums[q : q + 16, :].astype(jnp.bfloat16)
        part = pl.ds(r, 784)
        pltpu.make_async_copy(total.at[part], out_ref.at[part], out_sem).start()
    pltpu.make_async_copy(total, out_ref, out_sem).wait()


def ffn(gathered, wide, down):
    width, model_width = down.shape
    members = gathered.shape[0] // (2 * CAP)
    used = model_width // COLS * CAP
    stride = used // 8 * 8 + 7
    total = members * stride
    anywhere = pl.BlockSpec(memory_space=pl.ANY)
    return pl.pallas_call(
        ffn_kernel,
        out_shape=jax.ShapeDtypeStruct((total, COLS), jnp.bfloat16),
        in_specs=[anywhere] * 3,
        out_specs=anywhere,
        scratch_shapes=[
            pltpu.VMEM(gathered.shape, jnp.bfloat16),
            pltpu.VMEM(wide.shape, jnp.bfloat16),
            pltpu.VMEM(down.shape, jnp.bfloat16),
            pltpu.VMEM((members * CAP, model_width), jnp.bfloat16),
            pltpu.VMEM((total, COLS), jnp.float32),
            pltpu.VMEM((total, COLS), jnp.bfloat16),
            pltpu.SemaphoreType.DMA((7,)),
            pltpu.SemaphoreType.DMA((14,)),
            pltpu.SemaphoreType.DMA,
            pltpu.SemaphoreType.DMA,
        ],
        compiler_params=pltpu.CompilerParams(vmem_limit_bytes=60 << 20),
        cost_estimate=pl.CostEstimate(
            flops=6 * members * CAP * model_width * width,
            bytes_accessed=14 << 20,
            transcendentals=members * CAP * width,
        ),
    )(gathered, wide, down)


def body(tokens, route_ids, route_gates, gate_up, down_weight):
    model_width = tokens.shape[1]
    dp = lax.axis_index("dp")

    matches = route_ids == 0
    routed = jnp.any(matches, axis=1)
    weight = jnp.sum(jnp.where(matches, route_gates, 0.0), axis=1)
    places = jnp.cumsum(routed.astype(jnp.int32)) - 1
    capacity_ids = jnp.arange(CAP, dtype=jnp.int32)
    packing = (routed[None, :] & (places[None, :] == capacity_ids[:, None])).astype(jnp.bfloat16)
    packed = jnp.dot(packing, tokens, preferred_element_type=jnp.float32).astype(jnp.bfloat16)
    packed = jnp.concatenate((packed[:, : model_width // 2], packed[:, model_width // 2 :]), axis=0)

    shard = jnp.concatenate((gate_up[0], gate_up[1], down_weight.T), axis=1)
    packed, shard = lax.optimization_barrier((packed, shard))
    gathered = lax.all_gather(packed, "expert", axis=0, tiled=True)
    bundle = jnp.stack([shard] + [turn_plane(shard, s, False) for s in STEPS[1:]])
    own = jnp.stack([bundle] + [turn_plane(bundle, s, True) for s in STEPS[1:]])
    other = swap_cores(own)
    position = jnp.stack((dp // 8, dp // 2 % 4, dp % 2)).astype(jnp.int32)
    wide, down = place_weights(position, own, other, model_width)
    partial_value = ffn(gathered, wide, down)
    summed = lax.psum_scatter(partial_value, "expert", scatter_dimension=0, tiled=True)
    summed = lax.optimization_barrier(summed)
    blocks = model_width // COLS
    summed = summed[: blocks * CAP].reshape(blocks, CAP, COLS)
    summed = jnp.transpose(summed, (1, 0, 2)).reshape(CAP, model_width)
    selector = routed[:, None] & (places[:, None] == capacity_ids[None, :])
    scaled = jnp.where(selector, weight[:, None], 0.0)
    mixed = jnp.dot(
        scaled,
        summed.astype(jnp.float32),
        precision=lax.Precision.HIGHEST,
        preferred_element_type=jnp.float32,
    )
    return mixed.astype(jnp.bfloat16)


def solution(mesh):
    return jax.shard_map(
        body,
        mesh=mesh,
        in_specs=(
            P(("dp", "expert"), None),
            P(("dp", "expert"), None),
            P(("dp", "expert"), None),
            P(None, "dp", "expert"),
            P("expert", "dp"),
        ),
        out_specs=P(("dp", "expert"), None),
        check_vma=False,
    )
```
